128 devices in a mesh: gx: 16 (over x_hi, z, core), gy: 8 (over y, x_lo).
Axes of the slice: x: 4 (x_hi: 2, x_lo: 2; x = x_hi * 2 + x_lo), y: 4, z: 4, core: 2. Of those that a mesh axis runs over, the one named last changes fastest.
Arguments:
- initial_high_res_fields: bfloat16 [3, 16, 4096, 2048], P(None, None, 'gx', 'gy'), may hold values from -6 to 6
- anchors: int32 [1024, 512], P('gy'), may hold values from 0 to 8
- analysis_correction: float32 [3, 16, 1024, 512], P(None, 'gx', 'gy'), may hold values from -6 to 6
Outputs:
- predicted_high_res: bfloat16 [3, 16, 4096, 2048], P(None, None, 'gx', 'gy')
- propagated_perturb: float32 [3, 16, 1024, 512], P(None, 'gx', 'gy')
The draws below stay inside these ranges and needn't reach their ends.
Inputs may be any that keep to these rules, and one draw needn't show every extreme that they name: `anchors`: s selects the lower corner (s // 3, s % 3) of a 2 x 2 stencil inside the inner column's 4 x 4 block of fine columns.
All inputs are finite; a program needn't handle non-finite values.
Results may differ from the reference program's by a relative error of at most 0.0016.
Values may be sent and summed in bfloat16 or wider, within the bound.
No kernel may reach another device: no remote copies, remote signals or barrier semaphores. Data moves between devices by JAX's collectives and lax.ppermute only.
A program may use at most 192 MiB of HBM per device.

```python
import jax
import jax.numpy as jnp
from jax import lax

L = 16
NX = 4096
NY = 2048
NXC = 1024
NYC = 512


def set_ends(array, key, low, top_value):
    index_at = [jax.random.randint(jax.random.fold_in(key, axis), (), 0, length) for axis, length in enumerate(array.shape)]
    longest = array.shape.index(max(array.shape))
    next_to = index_at[:longest] + [(index_at[longest] + 1) % array.shape[longest]] + index_at[longest + 1:]
    return array.at[tuple(index_at)].set(low).at[tuple(next_to)].set(top_value)


def shard_levels(key, dims, split, least, top_value):
    loudness, own = 1.0, jax.random.fold_in(key, 6)
    for dim, parts in split:
        heights = jnp.exp(jax.random.uniform(jax.random.fold_in(own, dim), (parts,), jnp.float32, least / len(split), top_value / len(split)))
        loudness = loudness * jnp.repeat(heights, dims[dim] // parts).reshape([-1 if axis == dim else 1 for axis in range(len(dims))])
    return loudness


def noise(stream_key, extent, scale, bound, split=(), dtype=jnp.bfloat16):
    values = scale * jax.random.normal(stream_key, extent, jnp.float32)
    if split:
        values = values * shard_levels(stream_key, extent, split, -0.22, 0.18)
    return jnp.clip(values, -bound, bound).astype(dtype)


def setup_inputs(seed: int = 0) -> dict:
    splits = jax.random.split(jax.random.key(seed), 4)
    return {
        "initial_high_res_fields": noise(splits[0], (3, L, NX, NY), 1.0, 6.0, ((2, 16), (3, 8))),
        "anchors": set_ends(jax.random.randint(splits[1], (NXC, NYC), 0, 9), jax.random.fold_in(splits[1], 1), 0, 8).astype(jnp.int32),
        "analysis_correction": noise(splits[2], (3, L, NXC, NYC), 1.0, 6.0, ((1, 16), (2, 8)), jnp.float32),
    }


fine_grid_courant = 0.25
coarse_courant = 0.2


def north_diff(values):
    padded = jnp.pad(values, [(0, 0)] * (values.ndim - 1) + [(1, 1)])
    return padded[..., 2:] - padded[..., :-2]


def east_diff(values):
    return jnp.roll(values, -1, axis=-2) - jnp.roll(values, 1, axis=-2)


def fine_advect(level):
    values = level.astype(jnp.float32)
    eastward_neighbour = east_diff(values)
    northward_neighbour = north_diff(values)
    return (values - fine_grid_courant * (values[0:1] * eastward_neighbour + values[1:2] * northward_neighbour)).astype(jnp.bfloat16)


def average_into_cells(fine, anchors):
    leading = fine.shape[:-2]
    width_x = fine.shape[-2]
    width_y = fine.shape[-1]
    blocks = fine.reshape(leading + (width_x // 4, 4, width_y // 4, 4))
    result = jnp.zeros(leading + (width_x // 4, width_y // 4), jnp.float32)
    for anchor in range(9):
        shift_east = anchor // 3
        shift_north = anchor % 3
        average = 0.25 * (blocks[..., :, shift_east, :, shift_north].astype(jnp.float32)
                          + blocks[..., :, shift_east + 1, :, shift_north].astype(jnp.float32)
                          + blocks[..., :, shift_east, :, shift_north + 1].astype(jnp.float32)
                          + blocks[..., :, shift_east + 1, :, shift_north + 1].astype(jnp.float32))
        result = jnp.where(anchors == anchor, average, result)
    return result.astype(jnp.bfloat16)


def tangent_level(change, trajectory):
    basic = trajectory.astype(jnp.float32)
    return change - coarse_courant * (change[0:1] * east_diff(basic) + basic[0:1] * east_diff(change)
                                      + change[1:2] * north_diff(basic) + basic[1:2] * north_diff(change))


def reference(initial_high_res_fields, anchors, analysis_correction):
    def per_layer(pair):
        level, change = pair
        advanced = fine_advect(level)
        start = average_into_cells(level, anchors)
        later = average_into_cells(advanced, anchors)
        change = tangent_level(change, start)
        change = tangent_level(change, later)
        return advanced, change

    predicted_high_res, propagated_perturb = lax.map(per_layer, (jnp.moveaxis(initial_high_res_fields, 1, 0), jnp.moveaxis(analysis_correction, 1, 0)))
    return jnp.moveaxis(predicted_high_res, 0, 1), jnp.moveaxis(propagated_perturb, 0, 1)
```

```python
import jax
import jax.numpy as jnp
from jax import lax
from jax.experimental import pallas as pl
from jax.experimental.pallas import tpu as pltpu
from jax.sharding import PartitionSpec as P

fine_grid_courant = 0.25
coarse_courant = 0.2
F32 = jnp.float32
BF16 = jnp.bfloat16
AXES = ("gx", "gy")
VMEM_LIMIT = 56 * 1024 * 1024


def params():
    return pltpu.CompilerParams(vmem_limit_bytes=VMEM_LIMIT)


def iota(shape, dim):
    return lax.broadcasted_iota(jnp.int32, shape, dim)


def dot(a, b):
    return jnp.dot(a, b, preferred_element_type=F32)


def edges_kernel(pos, fine, pert_lo, pert_hi, rows_in, rows_out, cols_in, cols_out):
    even_x = pos[0] % 2 == 0
    even_y = pos[1] % 2 == 0
    step = pl.program_id(0) * pl.num_programs(1) + pl.program_id(1)
    count = fine.shape[1]
    width = fine.shape[3]
    side = iota((16, width), 0)
    column = iota((16, width), 1)
    pick = jnp.where(
        ((side == 0) & (column == 0)) | ((side == 1) & (column == width - 1)), 1.0, 0.0
    ).astype(BF16)
    base = pl.multiple_of(step * count, count)
    firsts, lasts, lefts, rights = [], [], [], []
    for p in range(count):
        head = fine[0, p, 0:16, :].astype(F32)
        tail = fine[0, p, width - 16 : width, :].astype(F32)
        firsts.append(head[0:1])
        lasts.append(tail[15:16])
        both = lax.dot_general(
            pick, fine[0, p], (((1,), (1,)), ((), ())), preferred_element_type=F32
        )
        lefts.append(both[0:1])
        rights.append(both[1:2])
    first = jnp.concatenate(firsts, axis=0)
    last = jnp.concatenate(lasts, axis=0)
    left = jnp.concatenate(lefts, axis=0)
    right = jnp.concatenate(rights, axis=0)
    rows_in[pl.ds(base, count), :] = jnp.where(even_x, last, first)
    rows_out[pl.ds(base, count), :] = jnp.where(even_x, first, last)
    cols_in[pl.ds(base, count), :] = jnp.where(even_y, right, left)
    cols_out[pl.ds(base, count), :] = jnp.where(even_y, left, right)

    @pl.when(step == 0)
    def _():
        planes = cols_in.shape[0] - 16
        cols_in[planes:, :] = jnp.zeros((16, width), F32)
        cols_out[planes:, :] = jnp.zeros((16, width), F32)
        for k in range(3):
            for r in range(2):
                lo = pert_lo[k, 0, r : r + 1, :]
                hi = pert_hi[k, 0, 6 + r : 7 + r, :]
                inner = jnp.where(even_y, hi, lo)
                outer = jnp.where(even_y, lo, hi)
                for h in range(2):
                    at = planes + (k * 2 + r) * 2 + h
                    cols_in[at : at + 1, :] = inner[:, h * width : (h + 1) * width]
                    cols_out[at : at + 1, :] = outer[:, h * width : (h + 1) * width]


def take_edges(pos, fine, pert):
    fields, levels, nx, ny = fine.shape
    count = 8
    planes = fields * levels
    whole = lambda n: pl.BlockSpec((n, ny), lambda k, s, pos: (0, 0))
    rows = pert.shape[2]
    return pl.pallas_call(
        edges_kernel,
        grid_spec=pltpu.PrefetchScalarGridSpec(
            num_scalar_prefetch=1,
            grid=(fields, levels // count),
            in_specs=[
                pl.BlockSpec((1, count, nx, ny), lambda k, s, pos: (k, s, 0, 0)),
                pl.BlockSpec((fields, 1, 8, pert.shape[3]), lambda k, s, pos: (0, 0, 0, 0)),
                pl.BlockSpec((fields, 1, 8, pert.shape[3]), lambda k, s, pos: (0, 0, rows // 8 - 1, 0)),
            ],
            out_specs=[whole(planes), whole(planes), whole(planes + 16), whole(planes + 16)],
        ),
        out_shape=[
            jax.ShapeDtypeStruct((planes, ny), F32),
            jax.ShapeDtypeStruct((planes, ny), F32),
            jax.ShapeDtypeStruct((planes + 16, ny), F32),
            jax.ShapeDtypeStruct((planes + 16, ny), F32),
        ],
        compiler_params=params(),
        name="edges",
    )(pos, fine, pert, pert)


def fine_kernel(
    pos, fine, rows_in, rows_out, cols_in, cols_out, anchors, ahead, coarse,
    north, east, mask, halo, pair_rows, pair_cols, stacked, stacked_lo,
):
    level = pl.program_id(0)
    levels = pl.num_programs(0)
    n = fine.shape[2]
    half = n // 8
    even_x = pos[0] % 2 == 0
    even_y = pos[1] % 2 == 0

    @pl.when(level == 0)
    def _():
        r = iota((n, n), 0)
        c = iota((n, n), 1)
        q = fine_grid_courant
        plain = jnp.where(r == c + 1, q, jnp.where(r == c - 1, -q, 0.0)).astype(BF16)
        east[...] = jnp.where(c == r + 1, q, jnp.where(c == r - 1, -q, 0.0)).astype(BF16)
        r2 = iota((128, n), 0)
        c2 = iota((128, n), 1)
        for k in range(3):
            at = k * levels
            north[k, 0:n, :] = plain
            north[k, n:, :] = jnp.where(
                (r2 == at) & (c2 == 0), -q, jnp.where((r2 == at + 64) & (c2 == n - 1), q, 0.0)
            ).astype(BF16)
        ri = iota((n // 4, n), 0)
        ci = iota((n // 4, n), 1)
        sums = jnp.where(ci // 4 == ri, 1.0, 0.0)
        pair_rows[...] = sums.astype(BF16)
        rp = iota((2 * n, 128), 0)
        cp = iota((2 * n, 128), 1)
        pair_cols[...] = jnp.where(
            (rp // n == cp // 64) & ((rp % n) // 4 == cp % 64), 0.25, 0.0
        ).astype(BF16)
        code = anchors[...]
        east_at = jnp.where(code >= 6, 2.0, jnp.where(code >= 3, 1.0, 0.0))
        north_at = code.astype(F32) - 3.0 * east_at
        rx = iota((n, n // 4), 0)
        cx = iota((n, n // 4), 1)
        up = jnp.where(rx // 4 == cx, 1.0, 0.0).astype(BF16)
        wide = sums.astype(BF16)

        def spread(x):
            return dot(dot(up, x.astype(BF16)).astype(BF16), wide)

        di = (r % 4).astype(F32) - spread(east_at)
        dj = (c % 4).astype(F32) - spread(north_at)
        inside = (di > -0.5) & (di < 1.5) & (dj > -0.5) & (dj < 1.5)
        mask[...] = jnp.where(inside, 1.0, 0.0).astype(BF16)
        left = jnp.where(even_y, cols_out[...], cols_in[...])
        right = jnp.where(even_y, cols_in[...], cols_out[...])
        left = jnp.where(pos[1] > 0, left, 0.0)
        right = jnp.where(pos[1] < pos[2] - 1, right, 0.0)
        halo[...] = jnp.concatenate([left, right], axis=0).T

    turned = pltpu.roll(halo[...], (128 - level) % 128, axis=1).astype(BF16)
    row_at = iota((8, n), 0)
    u = fine[0, 0].astype(F32)
    v = fine[1, 0].astype(F32)
    for k in range(3):
        own = fine[k, 0]
        toward_north = dot(jnp.concatenate([own, turned], axis=1), north[k])
        toward_east = dot(east[...], own)
        plane = k * levels + level
        inner = rows_in[pl.ds(plane, 1), :]
        outer = rows_out[pl.ds(plane, 1), :]
        low = jnp.where(even_x, outer, inner) * fine_grid_courant
        high = jnp.where(even_x, inner, outer) * fine_grid_courant
        toward_east = jnp.concatenate(
            [
                toward_east[0:8] - jnp.where(row_at == 0, low, 0.0),
                toward_east[8 : n - 8],
                toward_east[n - 8 : n] + jnp.where(row_at == 7, high, 0.0),
            ],
            axis=0,
        )
        value = u if k == 0 else v if k == 1 else own.astype(F32)
        moved = (value - (u * toward_east + v * toward_north)).astype(BF16)
        ahead[k, 0] = moved
        for state, field in ((0, own), (1, moved)):
            sums = dot(pair_rows[...], field * mask[...])
            high_part = sums.astype(BF16)
            low_part = (sums - high_part.astype(F32)).astype(BF16)
            at = (state * 3 + k) * half
            stacked[at : at + half, 0:n] = high_part[0:half]
            stacked[at : at + half, n : 2 * n] = high_part[half:]
            stacked_lo[at : at + half, 0:n] = low_part[0:half]
            stacked_lo[at : at + half, n : 2 * n] = low_part[half:]
    total = dot(stacked[...], pair_cols[...]) + dot(stacked_lo[...], pair_cols[...])
    coarse[0] = total.astype(BF16)


def fine_step(pos, fine, rows_in, rows_out, cols_in, cols_out, anchors):
    fields, levels, nx, ny = fine.shape
    whole = lambda a: pl.BlockSpec(a.shape, lambda l, pos: (0, 0))
    rows = 6 * nx // 8
    return pl.pallas_call(
        fine_kernel,
        grid_spec=pltpu.PrefetchScalarGridSpec(
            num_scalar_prefetch=1,
            grid=(levels,),
            in_specs=[
                pl.BlockSpec((fields, 1, nx, ny), lambda l, pos: (0, l, 0, 0)),
                whole(rows_in), whole(rows_out), whole(cols_in), whole(cols_out), whole(anchors),
            ],
            out_specs=[
                pl.BlockSpec((fields, 1, nx, ny), lambda l, pos: (0, l, 0, 0)),
                pl.BlockSpec((1, rows, 128), lambda l, pos: (l, 0, 0)),
            ],
            scratch_shapes=[
                pltpu.VMEM((3, nx + 128, ny), BF16),
                pltpu.VMEM((nx, nx), BF16),
                pltpu.VMEM((nx, ny), BF16),
                pltpu.VMEM((nx, 128), F32),
                pltpu.VMEM((nx // 4, nx), BF16),
                pltpu.VMEM((2 * ny, 128), BF16),
                pltpu.VMEM((rows, 2 * ny), BF16),
                pltpu.VMEM((rows, 2 * ny), BF16),
            ],
        ),
        out_shape=[
            jax.ShapeDtypeStruct(fine.shape, BF16),
            jax.ShapeDtypeStruct((levels, rows, 128), BF16),
        ],
        compiler_params=params(),
        name="fine",
    )(pos, fine, rows_in, rows_out, cols_in, cols_out, anchors)


def bundle_kernel(blocks, out):
    count, rows, _ = blocks.shape
    r = iota((32, rows), 0)
    c = iota((32, rows), 1)
    part = r // 2
    lower = jnp.where((r < 12) & (c == part * 32 + 30 + r % 2), 1.0, 0.0).astype(BF16)
    upper = jnp.where(
        (r >= 16) & (r < 28) & (c == (part - 8) * 32 + r % 2), 1.0, 0.0
    ).astype(BF16)
    for g in range(count // 2):
        out[g, 0:rows] = blocks[2 * g]
        out[g, rows : 2 * rows] = blocks[2 * g + 1]
        halo = dot(lower, blocks[(2 * g - 1) % count]) + dot(upper, blocks[(2 * g + 2) % count])
        out[g, 2 * rows :] = halo.astype(BF16)


def bundle(blocks):
    count, rows, lanes = blocks.shape
    return pl.pallas_call(
        bundle_kernel,
        out_shape=jax.ShapeDtypeStruct((count // 2, 2 * rows + 32, lanes), BF16),
        compiler_params=params(),
        name="bundle",
    )(blocks)


def tangent_kernel(pos, parts, pert, cols_in, cols_out, out, change, first, second):
    even_y = pos[1] % 2 == 0
    planes = cols_in.shape[0] - 16
    rows = pert.shape[2]
    width = pert.shape[3]
    deep = rows + 16
    half_width = width // 2
    lane = iota((32, 128), 1)
    near = lane < 64
    blank = jnp.zeros((8, width), F32)
    lower_rows = jnp.where(even_y, cols_out[planes:, :], cols_in[planes:, :])
    upper_rows = jnp.where(even_y, cols_in[planes:, :], cols_out[planes:, :])
    for k in range(3):
        change[k, 0:8, :] = blank
        change[k, rows + 8 :, :] = blank
        change[k, 8 : rows + 8, :] = pert[k, 0]
        for r in range(2):
            at = (k * 2 + r) * 2
            for h in range(2):
                span = slice(h * half_width, (h + 1) * half_width)
                change[k, 6 + r : 7 + r, span] = lower_rows[at + h : at + h + 1]
                change[k, rows + 8 + r : rows + 9 + r, span] = upper_rows[at + h : at + h + 1]
    for state, basic in ((0, first), (1, second)):
        for k in range(3):
            at = (state * 3 + k) * 32
            for m in range(width // 128):
                span = slice(m * 128, (m + 1) * 128)
                for a in range(2):
                    x = parts[2 * m, a * 192 + at : a * 192 + at + 32, :].astype(F32)
                    y = parts[2 * m + 1, a * 192 + at : a * 192 + at + 32, :].astype(F32)
                    row = 8 + a * 64
                    basic[k, row : row + 32, span] = jnp.where(near, x, pltpu.roll(y, 64, axis=1))
                    basic[k, row + 32 : row + 64, span] = jnp.where(near, pltpu.roll(x, 64, axis=1), y)
    for state, basic in ((0, first), (1, second)):
        for k in range(3):
            basic[k, 0:8, :] = blank
            basic[k, rows + 8 :, :] = blank
    for m in range(width // 128):
        span = slice(m * 128, (m + 1) * 128)
        x = parts[2 * m, 384:416, :].astype(F32)
        y = parts[2 * m + 1, 384:416, :].astype(F32)
        from_lower = jnp.where(near, pltpu.roll(x, 64, axis=1), y)
        from_upper = jnp.where(near, x, pltpu.roll(y, 64, axis=1))
        for state, basic in ((0, first), (1, second)):
            for k in range(3):
                at = (state * 3 + k) * 2
                basic[k, 6:8, span] = from_lower[at : at + 2]
                basic[k, rows + 8 : rows + 10, span] = from_upper[16 + at : 18 + at]
    column = iota((deep, width), 1)

    def east(x):
        return pltpu.roll(x, deep - 1, axis=0) - pltpu.roll(x, 1, axis=0)

    def north(x):
        ahead = jnp.where(column < width - 1, pltpu.roll(x, width - 1, axis=1), 0.0)
        behind = jnp.where(column > 0, pltpu.roll(x, 1, axis=1), 0.0)
        return ahead - behind

    for state, basic in ((0, first), (1, second)):
        d0 = change[0]
        d1 = change[1]
        b0 = basic[0]
        b1 = basic[1]
        for k in (2, 1, 0):
            d = change[k]
            b = basic[k]
            moved = d - coarse_courant * (d0 * east(b) + b0 * east(d) + d1 * north(b) + b1 * north(d))
            if state == 0:
                change[k] = moved
            else:
                out[k, 0] = moved[8 : rows + 8]


def tangent(pos, parts, pert, cols_in, cols_out):
    fields, _, rows, width = pert.shape
    vmem = pl.BlockSpec(memory_space=pltpu.VMEM)
    return pl.pallas_call(
        tangent_kernel,
        in_specs=[pl.BlockSpec(memory_space=pltpu.SMEM), vmem, vmem, vmem, vmem],
        out_specs=vmem,
        out_shape=jax.ShapeDtypeStruct(pert.shape, F32),
        scratch_shapes=[pltpu.VMEM((fields, rows + 16, width), F32)] * 3,
        compiler_params=params(),
        name="tangent",
    )(pos, parts, pert, cols_in, cols_out)


def inner_pairs(count):
    return [(i, i ^ 1) for i in range(count)]


def outer_pairs(count):
    return [(i, (i - 1 + 2 * (i % 2)) % count) for i in range(count)]


def on_device(fine, anchors, pert):
    nx = lax.axis_size("gx")
    ny = lax.axis_size("gy")
    x = lax.axis_index("gx")
    y = lax.axis_index("gy")
    pos = jnp.stack([x, y, jnp.int32(ny)]).astype(jnp.int32)
    cells_x = fine.shape[2] // 4
    cells_y = fine.shape[3] // 4
    column = lambda i: 2 * (i // 2 % 4) + i // 8
    served = lax.dynamic_slice(anchors, (x % 2 * cells_x, column(x) * cells_y), (cells_x, cells_y))
    route = [
        (i * ny + g, (2 * g + i % 2) * ny + column(i)) for i in range(nx) for g in range(ny)
    ]
    own_anchors = lax.ppermute(served, AXES, route)
    rows_in, rows_out, cols_in, cols_out = take_edges(pos, fine, pert)
    rows_in = lax.ppermute(rows_in, "gx", inner_pairs(nx))
    rows_out = lax.ppermute(rows_out, "gx", outer_pairs(nx))
    cols_in = lax.ppermute(cols_in, "gy", inner_pairs(ny))
    cols_out = lax.ppermute(cols_out, "gy", outer_pairs(ny))
    ahead, coarse = fine_step(pos, fine, rows_in, rows_out, cols_in, cols_out, own_anchors)
    coarse = lax.all_to_all(coarse, "gx", 0, 0, tiled=True)
    parts = lax.all_to_all(bundle(coarse), "gy", 0, 0, tiled=True)
    return ahead, tangent(pos, parts, pert, cols_in, cols_out)


def solution(mesh):
    placed = (P(None, None, "gx", "gy"), P("gy", None), P(None, "gx", "gy", None))
    return jax.shard_map(
        on_device,
        mesh=mesh,
        in_specs=placed,
        out_specs=(P(None, None, "gx", "gy"), P(None, "gx", "gy", None)),
        check_vma=False,
    )
```
